768 devices in a mesh: ctx: 64 (over x, y, core), tp: 12 (over z).
Axes of the slice: x: 4, y: 8, z: 12, core: 2. Of those that a mesh axis runs over, the one named last changes fastest.
Arguments:
- tokens: bfloat16 [16384, 2048], P('ctx'), may hold values from -12 to 12
- feature_weight: bfloat16 [2048, 384], P(None, 'tp'), may hold values from -0.125 to 0.125
- window_weight: bfloat16 [2048, 3072], P(None, 'tp'), may hold values from -1 to 1
- value_weight: bfloat16 [2048, 1536], P(None, 'tp'), may hold values from -0.125 to 0.125
- log_decay: float32 [16384, 12], P('ctx', 'tp'), may hold values from -1 to 0
- out_grad: bfloat16 [16384, 1536], P('ctx', 'tp'), may hold values from -6 to 6
Outputs:
- attended: bfloat16 [16384, 1536], P('ctx', 'tp')
- input_grad: bfloat16 [16384, 2048], P('ctx')
The draws below stay inside these ranges and needn't reach their ends.
All inputs are finite; a program needn't handle non-finite values.
Results may differ from the reference program's by a relative error of at most 0.012.
The reference program's roundings to bfloat16 on the way count: a program that leaves them out, or rounds other values in their place, can miss the bound.
Values may be sent and summed in bfloat16 or wider, within the bound.
A program may use at most 64 MiB of HBM per device.

```python
import math
from functools import partial
import jax
import jax.numpy as jnp
from jax import lax

D = 2048
DH = 128
F = 16
WINDOW = 1024
ROWS = 256
ATTN_GROUPS = 12
PHI = 273
SEQ_SPAN = 16384


def draw_tokens(key, part):
    stochastic_seed_parts = jax.random.split(key, 2)
    offsets = jnp.clip(jax.random.normal(stochastic_seed_parts[1], (SEQ_SPAN // ROWS, D), jnp.float32), -3.0, 3.0) * 0.7
    shifted = jnp.repeat(offsets, ROWS, axis=0)
    basis = jnp.clip(jax.random.normal(stochastic_seed_parts[0], (SEQ_SPAN, D), jnp.float32), -4.0, 4.0)
    return (basis + shifted).astype(jnp.bfloat16)


def draw_window_weight(key, part):
    stochastic_seed_parts = jax.random.split(key, 2)
    scale = D ** (-0.5)
    query_part = jnp.clip(jax.random.normal(stochastic_seed_parts[0], (D, ATTN_GROUPS, 1, DH), jnp.float32), -6.0, 6.0)
    key_part = jnp.clip(jax.random.normal(stochastic_seed_parts[1], (D, ATTN_GROUPS, 1, DH), jnp.float32), -6.0, 6.0)
    joined = jnp.concatenate([query_part, key_part], axis=2) * scale
    return joined.reshape(D, 2 * DH * ATTN_GROUPS).astype(jnp.bfloat16)


def draw_log_decay(key, part):
    stochastic_seed_parts = jax.random.split(key, 6)
    portion = 0.5
    slow_heads = jax.random.uniform(stochastic_seed_parts[0], (1, ATTN_GROUPS), jnp.float32) < portion
    slow_rate = jax.random.uniform(stochastic_seed_parts[1], (1, ATTN_GROUPS), jnp.float32, 0.1, 0.5) * (math.log(10.0) / (1.25 * SEQ_SPAN))
    fast_rate = jax.random.uniform(stochastic_seed_parts[2], (1, ATTN_GROUPS), jnp.float32, 1.0 / 50.0, 1.0 / 30.0)
    chosen_speed = jnp.where(slow_heads, slow_rate, fast_rate)
    texture_jaggedness = jax.random.uniform(stochastic_seed_parts[3], (SEQ_SPAN, ATTN_GROUPS), jnp.float32, 0.5, 2.0)
    spike_occurrences = jax.random.uniform(stochastic_seed_parts[4], (SEQ_SPAN, ATTN_GROUPS), jnp.float32) < 3.0 / SEQ_SPAN
    objective_trace = jnp.log(jax.random.uniform(stochastic_seed_parts[5], (SEQ_SPAN, ATTN_GROUPS), jnp.float32, 0.6, 0.8))
    return -chosen_speed * texture_jaggedness + jnp.where(spike_occurrences, objective_trace, 0.0)


def shard_levels(rng, extent, shards, low, high):
    gain = 1.0
    for axis_at, shards_of in shards:
        draws = jax.random.uniform(jax.random.fold_in(jax.random.fold_in(rng, 6), axis_at), (shards_of,), jnp.float32, low / len(shards), high / len(shards))
        gain = gain * jnp.repeat(jnp.exp(draws), extent[axis_at] // shards_of).reshape((-1,) + (1,) * (len(extent) - 1 - axis_at))
    return gain


def normal_values(own_key, dims, spread, reach, cuts=(), kind=jnp.bfloat16):
    entries = spread * jax.random.normal(own_key, dims, jnp.float32)
    if cuts:
        entries = entries * shard_levels(own_key, dims, cuts, -0.22, 0.18)
    return jnp.clip(entries, -reach, reach).astype(kind)


def setup_inputs(seed: int = 0) -> dict:
    key_of = jax.random.split(jax.random.key(seed), 7)
    return {
        "tokens": draw_tokens(jax.random.fold_in(key_of[6], 71), 0),
        "feature_weight": normal_values(key_of[1], (D, 2 * F * ATTN_GROUPS), D ** -0.5, 0.125, ((1, 12),)),
        "window_weight": draw_window_weight(jax.random.fold_in(key_of[6], 71), 0),
        "value_weight": normal_values(key_of[3], (D, DH * ATTN_GROUPS), D ** -0.5, 0.125, ((1, 12),)),
        "log_decay": draw_log_decay(jax.random.fold_in(key_of[6], 71), 0),
        "out_grad": normal_values(key_of[5], (SEQ_SPAN, DH * ATTN_GROUPS), 1.0, 6.0, ((0, 64), (1, 12))),
    }


precise = lax.Precision.HIGHEST

def feature_map(vectors):
    row_count = vectors.shape[0]
    feat_width = vectors.shape[1]
    square = (vectors[:, :, None] * vectors[:, None, :]).reshape(row_count, feat_width * feat_width) * 0.5 ** 0.5
    return jnp.concatenate([square, vectors, jnp.ones((row_count, 1), jnp.float32)], axis=1)

def linear_part(query_feat, query_cum, query_pos, key_feat, key_cum, key_pos, value_rows, state_num, state_den):
    products = jnp.dot(query_feat, key_feat.T, precision=precise)
    kernel = 1.0 + products + 0.5 * products * products
    causal = key_pos[None, :] <= query_pos[:, None]
    decay_table = jnp.exp(jnp.where(causal, query_cum[:, None] - key_cum[None, :], -jnp.inf))
    weights = kernel * decay_table
    lifted = feature_map(query_feat)
    growth = jnp.exp(query_cum)
    numerator = jnp.dot(weights, value_rows, precision=precise) + growth[:, None] * jnp.dot(lifted, state_num, precision=precise)
    denominator = lax.optimization_barrier(jnp.sum(weights, axis=1)) + growth * jnp.dot(lifted, state_den, precision=precise)
    return numerator / denominator[:, None]

def window_part(queries, query_pos, key_rows, key_values, key_pos):
    scores = jnp.dot(queries, key_rows.T, precision=precise) * DH ** (-0.5)
    allowed = (key_pos[None, :] <= query_pos[:, None]) & (query_pos[:, None] - key_pos[None, :] < WINDOW) & (key_pos[None, :] >= 0)
    scores = jnp.where(allowed, scores, -jnp.inf)
    row_max = lax.optimization_barrier(jnp.max(scores, axis=1, keepdims=True))
    exponent = jnp.exp(scores - row_max)
    return jnp.dot(exponent, key_values, precision=precise) / lax.optimization_barrier(jnp.sum(exponent, axis=1, keepdims=True))

def head_forward(features, window, values, log_rates):
    feat_scale = F ** (-0.25)
    query_feat = features[:, :F] * feat_scale
    key_feat = features[:, F:] * feat_scale
    queries = window[:, :DH]
    pad_keys = jnp.concatenate([jnp.zeros((WINDOW, DH), jnp.float32), window[:, DH:]], axis=0)
    pad_values = jnp.concatenate([jnp.zeros((WINDOW, DH), jnp.float32), values], axis=0)
    local_pos = jnp.arange(ROWS, dtype=jnp.int32)
    window_pos = jnp.arange(WINDOW + ROWS, dtype=jnp.int32)

    def advance(states, block_index):
        state_num, state_den = states
        first_row = block_index * ROWS
        block_query = lax.dynamic_slice_in_dim(query_feat, first_row, ROWS, 0)
        block_key = lax.dynamic_slice_in_dim(key_feat, first_row, ROWS, 0)
        block_values = lax.dynamic_slice_in_dim(values, first_row, ROWS, 0)
        cumulative = jnp.cumsum(lax.dynamic_slice_in_dim(log_rates, first_row, ROWS, 0))
        linear = linear_part(block_query, cumulative, local_pos, block_key, cumulative, local_pos, block_values, state_num, state_den)
        windowed = window_part(lax.dynamic_slice_in_dim(queries, first_row, ROWS, 0), first_row + local_pos, lax.dynamic_slice_in_dim(pad_keys, first_row, WINDOW + ROWS, 0), lax.dynamic_slice_in_dim(pad_values, first_row, WINDOW + ROWS, 0), first_row - WINDOW + window_pos)
        tail_decay = jnp.exp(cumulative[-1] - cumulative)
        phi_keys = feature_map(block_key) * tail_decay[:, None]
        new_num = jnp.exp(cumulative[-1]) * state_num + jnp.dot(phi_keys.T, block_values, precision=precise)
        new_den = jnp.exp(cumulative[-1]) * state_den + lax.optimization_barrier(jnp.sum(phi_keys, axis=0))
        return ((new_num, new_den), linear + windowed)
    initial = (jnp.zeros((PHI, DH), jnp.float32), jnp.zeros((PHI,), jnp.float32))
    block_count = SEQ_SPAN // ROWS
    _, outputs = lax.scan(advance, initial, jnp.arange(block_count, dtype=jnp.int32))
    return outputs.reshape(SEQ_SPAN, DH)

def reference(tokens, feature_weight, window_weight, value_weight, log_decay, out_grad):
    features = jnp.dot(tokens, feature_weight, preferred_element_type=jnp.float32).astype(jnp.bfloat16)
    window = jnp.dot(tokens, window_weight, preferred_element_type=jnp.float32).astype(jnp.bfloat16)
    values = jnp.dot(tokens, value_weight, preferred_element_type=jnp.float32).astype(jnp.bfloat16)

    def per_head(head_index):
        feat_cols = lax.dynamic_slice_in_dim(features, head_index * (2 * F), 2 * F, 1).astype(jnp.float32)
        win_cols = lax.dynamic_slice_in_dim(window, head_index * (2 * DH), 2 * DH, 1).astype(jnp.float32)
        val_cols = lax.dynamic_slice_in_dim(values, head_index * DH, DH, 1).astype(jnp.float32)
        head_rates = lax.dynamic_slice_in_dim(log_decay, head_index, 1, 1)[:, 0]
        cotangent = lax.dynamic_slice_in_dim(out_grad, head_index * DH, DH, 1).astype(jnp.float32)
        result, pullback = jax.vjp(partial(head_forward, log_rates=head_rates), feat_cols, win_cols, val_cols)
        gradients = pullback(cotangent)
        return (result.astype(jnp.bfloat16), gradients[0].astype(jnp.bfloat16), gradients[1].astype(jnp.bfloat16), gradients[2].astype(jnp.bfloat16))
    head_out, grad_feat, grad_win, grad_val = lax.map(per_head, jnp.arange(ATTN_GROUPS, dtype=jnp.int32))
    attended = jnp.transpose(head_out, (1, 0, 2)).reshape(SEQ_SPAN, ATTN_GROUPS * DH)
    grad_feat = jnp.transpose(grad_feat, (1, 0, 2)).reshape(SEQ_SPAN, ATTN_GROUPS * 2 * F)
    grad_win = jnp.transpose(grad_win, (1, 0, 2)).reshape(SEQ_SPAN, ATTN_GROUPS * 2 * DH)
    grad_val = jnp.transpose(grad_val, (1, 0, 2)).reshape(SEQ_SPAN, ATTN_GROUPS * DH)
    input_grad = jnp.dot(grad_feat, feature_weight.T, preferred_element_type=jnp.float32) + jnp.dot(grad_win, window_weight.T, preferred_element_type=jnp.float32) + jnp.dot(grad_val, value_weight.T, preferred_element_type=jnp.float32)
    return (attended, input_grad.astype(jnp.bfloat16))
```

```python
import jax
import jax.numpy as jnp
from jax import lax
from jax.experimental import pallas as pl
from jax.experimental.pallas import tpu as pltpu
from jax.sharding import PartitionSpec as P

F32 = jnp.float32
BF = jnp.bfloat16
MESH = pl.DeviceIdType.MESH
ROWS = 256
DH = 128
D = 2048
FEATS = 256
HALF = 96
SHARD = 352
SUB = 176
NEG = -1e30


def dot(a, b, ca, cb, precision=None):
    return lax.dot_general(
        a, b, (((ca,), (cb,)), ((), ())), precision=precision, preferred_element_type=F32
    )


def nn(a, b):
    return dot(a, b, 1, 0)


def nt(a, b):
    return dot(a, b, 1, 1)


def tn(a, b):
    return dot(a, b, 0, 0)


def iota(shape, dim):
    return lax.broadcasted_iota(jnp.int32, shape, dim)


def selections(offset):
    row = iota((32, FEATS), 0) - offset
    f = iota((32, FEATS), 1)
    low = f & 15
    pair = f < 136
    linear = (f >= 144) & (f < 160)
    first = (row == low) & (pair | linear)
    second = (row == ((low + (f >> 4)) & 15)) & pair
    return (
        jnp.where(first, 1.0, 0.0).astype(BF),
        jnp.where(second, 1.0, 0.0).astype(BF),
    )


def rate_of(block):
    return block[84:85] + block[85:86]


def with_rate(block, rate):
    row = iota((HALF, DH), 0)
    high = rate.astype(BF).astype(F32)
    return jnp.where(row == 84, high, jnp.where(row == 85, rate - high, block)).astype(BF)


def kernel_body(ctx_n, tp_n):
    ynum, xnum = 8, ctx_n // 16
    links = tp_n // 2
    back = tp_n - 1 - links

    def body(
        tok_h, wf_h, ww_h, wv_h, ld_ref, og_ref,
        att_ref, ig_ref,
        tok, wf, ww, wv, insem,
        kv, kvs, kvr,
        msg, pm, hb, yb, rb, xb, pb, po,
        cs, cr, ys, yr, xs, xr,
        dkv0, dkv2, dkv4, dsend, prt, m2, m1, r2, r1, gs, gr,
        part, res, rsb, rss, rsr, ags, agr,
    ):
        i = lax.axis_index("ctx")
        z = lax.axis_index("tp")
        c = lax.rem(i, 2)
        chip = i // 2
        y = lax.rem(chip, ynum)
        x = chip // ynum
        partner = i + 1 - 2 * c
        after = lax.rem(i + 2, ctx_n)
        before = lax.rem(i + ctx_n - 2, ctx_n)
        up = lax.rem(z + 1, tp_n)
        down = lax.rem(z + tp_n - 1, tp_n)

        def y_peer(k):
            return (x * ynum + lax.rem(y + k + ynum, ynum)) * 2 + c

        def x_peer(k):
            return (lax.rem(x + k + xnum, xnum) * ynum + y) * 2 + c

        loads = [
            pltpu.make_async_copy(a, b, insem.at[n])
            for n, (a, b) in enumerate(((tok_h, tok), (wf_h, wf), (wv_h, wv), (ww_h, ww)))
        ]
        for one in loads:
            one.start()
        barrier = pltpu.get_barrier_semaphore()
        peers = [{"ctx": partner}, {"ctx": after}, {"ctx": before}, {"tp": up}, {"tp": down}]
        peers += [{"ctx": y_peer(k)} for k in range(1, ynum)]
        peers += [{"ctx": x_peer(k)} for k in range(1, xnum)]
        for peer in peers:
            pl.semaphore_signal(barrier, inc=1, device_id=peer, device_id_type=MESH)

        def send(src, dst, ssem, rsem, peer):
            copy = pltpu.make_async_remote_copy(
                src_ref=src, dst_ref=dst, send_sem=ssem, recv_sem=rsem,
                device_id=peer, device_id_type=MESH,
            )
            copy.start()
            return copy

        ld = jnp.broadcast_to(ld_ref[...], (DH, ROWS))
        tri = jnp.where(iota((ROWS, ROWS), 1) <= iota((ROWS, ROWS), 0), 1.0, 0.0).astype(F32)
        cum = dot(tri, ld, 1, 1, lax.Precision.HIGHEST)
        cum_row = dot(ld[0:8], tri, 1, 1, lax.Precision.HIGHEST)[0:1]
        total = cum[ROWS - 1 : ROWS]
        growth = jnp.exp(cum)
        tail = jnp.exp(total - cum)
        causal = iota((ROWS, ROWS), 1) <= iota((ROWS, ROWS), 0)
        decay = jnp.exp(jnp.where(causal, cum[:, 0:1] - cum_row, NEG))
        tail1 = tail[:, 0:1]
        growth1 = growth[:, 0:1]

        aq, bq = selections(0)
        ak, bk = selections(16)
        lane = iota((1, FEATS), 1)
        a0 = jnp.where(lane == 136, 1.0, 0.0)
        b0 = jnp.where((lane == 136) | ((lane >= 144) & (lane < 160)), 1.0, 0.0)
        wq = jnp.where(lane < 16, 0.5, 1.0)

        for n in range(3):
            loads[n].wait()
        toks = tok[...]
        fs = (nn(toks, wf[...]).astype(BF).astype(F32) * 0.5).astype(BF)
        val = nn(toks, wv[...]).astype(BF)
        og = og_ref[...]
        ka = nn(fs, ak) + a0
        kb = nn(fs, bk) + b0
        phik = ka * kb * tail1
        phik_b = phik.astype(BF)

        def message(num, den):
            row = iota((16, DH), 0)
            high = total.astype(BF).astype(F32)
            extra = jnp.where(row == 0, den[:, :DH], 0.0)
            extra = jnp.where(row == 1, den[:, DH:], extra)
            extra = jnp.where(row == 4, high, extra)
            extra = jnp.where(row == 5, total - high, extra).astype(BF)
            return jnp.concatenate(
                [num[0:80].astype(BF), extra, num[80:160].astype(BF), extra], axis=0
            )

        def scan_stages(n, cc, yy, xx, sign):
            state = {}

            def start(num, den):
                msg[n] = message(num, den)
                state["a"] = send(msg.at[n], pm.at[n], cs.at[2 * n], cr.at[2 * n], {"ctx": partner})

            def stage_y():
                state["a"].wait()
                own = msg[n, pl.ds(pl.multiple_of(c * HALF, 16), HALF)].astype(F32)
                other = pm[n, pl.ds(pl.multiple_of(c * HALF, 16), HALF)].astype(F32)
                to, tp_ = rate_of(own), rate_of(other)
                first = cc == 0
                both = jnp.where(first, jnp.exp(tp_), 1.0) * own
                both = both + jnp.where(first, 1.0, jnp.exp(to)) * other
                hb[n] = with_rate(both, to + tp_)
                state["y"] = [
                    send(hb.at[n], yb.at[n, k], ys.at[n, k], yr.at[n, k], {"ctx": y_peer(sign * k)})
                    for k in range(1, ynum)
                ]

            def stage_x():
                prefix = jnp.zeros((HALF, DH), F32)
                suffix = jnp.zeros((HALF, DH), F32)
                d1 = jnp.zeros((1, DH), F32)
                d2 = jnp.zeros((1, DH), F32)
                for k in range(1, ynum):
                    state["y"][k - 1].wait_recv()
                    block = yb[n, k].astype(F32)
                    rate = rate_of(block)
                    early = k <= yy
                    prefix = prefix + jnp.where(early, jnp.exp(d1), 0.0) * block
                    suffix = suffix + jnp.where(early, 0.0, jnp.exp(d2)) * block
                    d1 = d1 + jnp.where(early, rate, 0.0)
                    d2 = d2 + jnp.where(early, 0.0, rate)
                own = hb[n].astype(F32)
                rate = rate_of(own)
                row_sum = jnp.exp(d2) * (jnp.exp(rate) * prefix + own) + suffix
                rb[n] = with_rate(row_sum, d1 + rate + d2)
                state["x"] = [
                    send(rb.at[n], xb.at[n, k], xs.at[n, k], xr.at[n, k], {"ctx": x_peer(sign * k)})
                    for k in range(1, xnum)
                ]
                state["prefix"], state["d1"] = prefix, d1

            def stage_pair():
                rows = jnp.zeros((HALF, DH), F32)
                dx = jnp.zeros((1, DH), F32)
                for k in range(1, xnum):
                    state["x"][k - 1].wait_recv()
                    block = xb[n, k].astype(F32)
                    early = k <= xx
                    rows = rows + jnp.where(early, jnp.exp(dx), 0.0) * block
                    dx = dx + jnp.where(early, rate_of(block), 0.0)
                pb[n] = (state["prefix"] + jnp.exp(state["d1"]) * rows).astype(BF)
                state["b"] = send(
                    pb.at[n], po.at[n], cs.at[2 * n + 1], cr.at[2 * n + 1], {"ctx": partner}
                )

            def finish():
                state["b"].wait()
                for one in state["y"] + state["x"]:
                    one.wait_send()
                mine, theirs = pb[n].astype(F32), po[n].astype(F32)
                low = jnp.where(c == 0, mine, theirs)
                high = jnp.where(c == 0, theirs, mine)
                near = pm[n].astype(F32)
                rate = rate_of(near[0:HALF])
                second = cc == 1
                scale = jnp.where(second, jnp.exp(rate), 1.0)
                take = jnp.where(second, 1.0, 0.0)
                num = jnp.concatenate(
                    [
                        scale * low[0:80] + take * near[0:80],
                        scale * high[0:80] + take * near[96:176],
                        jnp.zeros((FEATS - 160, DH), F32),
                    ],
                    axis=0,
                ).astype(BF)
                dens = scale * low[80:82] + take * near[80:82]
                return num, jnp.concatenate([dens[0:1], dens[1:2]], axis=1)

            return start, stage_y, stage_x, stage_pair, finish

        fwd = scan_stages(0, c, y, x, 1)
        rev = scan_stages(1, 1 - c, ynum - 1 - y, xnum - 1 - x, -1)

        pl.semaphore_wait(barrier, len(peers))
        fwd[0](tn(phik_b, val), jnp.sum(phik, axis=0, keepdims=True))

        loads[3].wait()
        win = nn(toks, ww[...]).astype(BF)
        wquery = win[:, :DH]
        kv[4] = jnp.concatenate([win[:, DH:], val], axis=1)
        hop1 = send(kv.at[4], kv.at[2], kvs.at[0], kvr.at[0], {"ctx": after})

        lane32 = iota((1, 32), 1)
        perm = jnp.where(
            iota((32, 32), 0) == ((iota((32, 32), 1) + 16) & 31), 1.0, 0.0
        ).astype(BF)
        swapped = nn(fs, perm)
        fq = jnp.where(lane32 < 16, fs.astype(F32), 0.0).astype(BF)
        ks = jnp.where(lane32 < 16, swapped, 0.0).astype(BF)
        qs = jnp.where(lane32 < 16, 0.0, swapped).astype(BF)
        prod = nt(fq, ks)
        weights = (1.0 + prod + 0.5 * prod * prod) * decay
        weights_b = weights.astype(BF)
        qa = nn(fs, aq) + a0
        qb = nn(fs, bq) + b0
        phiq = qa * qb * wq
        phiq_b = phiq.astype(BF)

        fwd[1]()
        num_in = nn(weights_b, val)
        den_in = jnp.sum(weights, axis=1, keepdims=True)
        hop1.wait()
        hop2 = send(kv.at[2], kv.at[0], kvs.at[1], kvr.at[1], {"ctx": after})
        pair1 = send(kv.at[4 - 2 * c], kv.at[3], kvs.at[2], kvr.at[2], {"ctx": partner})

        fwd[2]()
        hop2.wait()
        pair2 = send(kv.at[2 - 2 * c], kv.at[1], kvs.at[3], kvr.at[3], {"ctx": partner})
        fwd[3]()
        state_num, state_den = fwd[4]()

        num = num_in + growth * nn(phiq_b, state_num)
        den = den_in + growth1 * jnp.sum(phiq * state_den, axis=1, keepdims=True)
        inv = 1.0 / den
        linear = num * inv
        ogf = og.astype(F32)
        along = jnp.sum(ogf * linear, axis=1, keepdims=True)
        dnum = ogf * inv
        gden = growth1 * (-along * inv)
        gnum = (growth * dnum).astype(BF)
        rev[0](tn(phiq_b, gnum), jnp.sum(phiq * gden, axis=0, keepdims=True))

        pair1.wait()
        pair2.wait()
        scale = DH**-0.5
        scores = []
        for d in range(5):
            s = nt(wquery, kv[4 - d, :, :DH]) * scale
            if d == 0:
                s = jnp.where(causal, s, NEG)
            elif d == 4:
                s = jnp.where(causal | (i < d), NEG, s)
            else:
                s = jnp.where(i < d, NEG, s)
            scores.append(s)
        top = jnp.max(scores[0], axis=1, keepdims=True)
        for s in scores[1:]:
            top = jnp.maximum(top, jnp.max(s, axis=1, keepdims=True))
        probs = [jnp.exp(s - top) for s in scores]
        mass = jnp.sum(probs[0], axis=1, keepdims=True)
        for p in probs[1:]:
            mass = mass + jnp.sum(p, axis=1, keepdims=True)
        imass = 1.0 / mass
        windowed = jnp.zeros((ROWS, DH), F32)
        for d in range(5):
            windowed = windowed + nn(probs[d].astype(BF), kv[4 - d, :, DH:])
        windowed = windowed * imass
        att_ref[...] = (linear + windowed).astype(BF)
        rev[1]()
        delta = jnp.sum(ogf * windowed, axis=1, keepdims=True)
        dquery = jnp.zeros((ROWS, DH), F32)
        local_dv = None
        for d in (1, 3, 4, 2, 0):
            dp = nt(og, kv[4 - d, :, DH:])
            if d == 0:
                local_dv = dp
            p = probs[d] * imass
            ds = (p * (dp - delta) * scale).astype(BF)
            dquery = dquery + nn(ds, kv[4 - d, :, :DH])
            both = jnp.concatenate([tn(ds, wquery), tn(p.astype(BF), og)], axis=1)
            if d == 1:
                dsend[0] = both.astype(BF)
            elif d == 3:
                dsend[1] = both.astype(BF)
                swap = send(dsend, prt, gs.at[0], gr.at[0], {"ctx": partner})
            else:
                {0: dkv0, 2: dkv2, 4: dkv4}[d][...] = both
        rev[2]()

        swap.wait()
        m2[...] = (dkv4[...] + jnp.where(c == 1, prt[1].astype(F32), 0.0)).astype(BF)
        ret2 = send(m2, r2, gs.at[1], gr.at[1], {"ctx": before})

        dw = (local_dv - along) * inv
        dprod = (dw * decay * (1.0 + prod)).astype(BF)
        dphiq = (nt(gnum, state_num) + gden * state_den) * wq
        dfeat = nn(dprod, ks) + tn(dprod, qs)
        dfeat = dfeat + nt((dphiq * qb).astype(BF), aq) + nt((dphiq * qa).astype(BF), bq)
        dval = tn(weights_b, dnum.astype(BF))

        rev[3]()
        ret2.wait()
        near = jnp.where(c == 0, prt[1].astype(F32), prt[0].astype(F32))
        m1[...] = (dkv2[...] + near + r2[...].astype(F32)).astype(BF)
        ret1 = send(m1, r1, gs.at[2], gr.at[2], {"ctx": before})
        back_num, back_den = rev[4]()

        dphik = tail1 * (nt(val, back_num) + back_den)
        dfeat = dfeat + nt((dphik * kb).astype(BF), ak) + nt((dphik * ka).astype(BF), bk)
        dval = dval + nn(phik_b, back_num)
        gfeat = (0.5 * dfeat).astype(BF)
        ret1.wait()
        whole = dkv0[...] + jnp.where(c == 0, prt[0].astype(F32), 0.0) + r1[...].astype(F32)
        gwin = jnp.concatenate([dquery, whole[:, :DH]], axis=1).astype(BF)
        gval = (dval + whole[:, DH:]).astype(BF)

        for j in range(D // DH):
            cut = slice(j * DH, (j + 1) * DH)
            term = nt(gwin, ww[cut]) + nt(gval, wv[cut]) + nt(gfeat, wf[cut])
            part[j * ROWS : (j + 1) * ROWS] = term.astype(BF)
        tail_rows = tp_n * SHARD - D // DH * ROWS
        part[D // DH * ROWS :] = jnp.zeros((tail_rows, DH), BF)

        def rows_of(shard, h):
            at = lax.rem(shard + 2 * tp_n, tp_n) * SHARD + h * SUB
            return pl.ds(pl.multiple_of(at, 16), SUB)

        rs = {}
        ag = {}
        for t in range(1, links + 1):
            for h in range(2):
                for way in range(2):
                    if way == 1 and t > back:
                        continue
                    shard = z + links + 1 - t if way == 0 else z - back - 1 + t
                    if t == 1:
                        src = part.at[rows_of(shard, h)]
                    else:
                        rs[way, t - 1, h].wait_recv()
                        slot = rsb.at[way, t - 1, h]
                        slot[...] = (
                            slot[...].astype(F32) + part[rows_of(shard, h)].astype(F32)
                        ).astype(BF)
                        src = slot
                    rs[way, t, h] = send(
                        src, rsb.at[way, t, h], rss.at[way, t, h], rsr.at[way, t, h],
                        {"tp": up if way == 0 else down},
                    )
        for t in range(1, links + 1):
            for h in range(2):
                if t == 1:
                    rs[0, links, h].wait_recv()
                    rs[1, back, h].wait_recv()
                    res[rows_of(z, h)] = (
                        part[rows_of(z, h)].astype(F32)
                        + rsb[0, links, h].astype(F32)
                        + rsb[1, back, h].astype(F32)
                    ).astype(BF)
                for way in range(2):
                    if way == 1 and t > back:
                        continue
                    shard = z - t + 1 if way == 0 else z + t - 1
                    if t > 1:
                        ag[way, t - 1, h].wait_recv()
                    at = rows_of(shard, h)
                    ag[way, t, h] = send(
                        res.at[at], res.at[at], ags.at[way, t, h], agr.at[way, t, h],
                        {"tp": up if way == 0 else down},
                    )
        for h in range(2):
            ag[0, links, h].wait_recv()
            ag[1, back, h].wait_recv()
        for one in list(rs.values()) + list(ag.values()):
            one.wait_send()
        for j in range(D // DH):
            ig_ref[:, j * DH : (j + 1) * DH] = res[j * ROWS : (j + 1) * ROWS]

    scratch = [
        pltpu.VMEM((ROWS, D), BF), pltpu.VMEM((D, 32), BF),
        pltpu.VMEM((D, 2 * DH), BF), pltpu.VMEM((D, DH), BF),
        pltpu.SemaphoreType.DMA((4,)),
        pltpu.VMEM((5, ROWS, 2 * DH), BF),
        pltpu.SemaphoreType.DMA((4,)), pltpu.SemaphoreType.DMA((4,)),
        pltpu.VMEM((2, 2 * HALF, DH), BF), pltpu.VMEM((2, 2 * HALF, DH), BF),
        pltpu.VMEM((2, HALF, DH), BF), pltpu.VMEM((2, 8, HALF, DH), BF),
        pltpu.VMEM((2, HALF, DH), BF), pltpu.VMEM((2, 4, HALF, DH), BF),
        pltpu.VMEM((2, HALF, DH), BF), pltpu.VMEM((2, HALF, DH), BF),
        pltpu.SemaphoreType.DMA((4,)), pltpu.SemaphoreType.DMA((4,)),
        pltpu.SemaphoreType.DMA((2, 8)), pltpu.SemaphoreType.DMA((2, 8)),
        pltpu.SemaphoreType.DMA((2, 4)), pltpu.SemaphoreType.DMA((2, 4)),
        pltpu.VMEM((ROWS, 2 * DH), F32), pltpu.VMEM((ROWS, 2 * DH), F32),
        pltpu.VMEM((ROWS, 2 * DH), F32),
        pltpu.VMEM((2, ROWS, 2 * DH), BF), pltpu.VMEM((2, ROWS, 2 * DH), BF),
        pltpu.VMEM((ROWS, 2 * DH), BF), pltpu.VMEM((ROWS, 2 * DH), BF),
        pltpu.VMEM((ROWS, 2 * DH), BF), pltpu.VMEM((ROWS, 2 * DH), BF),
        pltpu.SemaphoreType.DMA((3,)), pltpu.SemaphoreType.DMA((3,)),
        pltpu.VMEM((tp_n * SHARD, DH), BF), pltpu.VMEM((tp_n * SHARD, DH), BF),
        pltpu.VMEM((2, links + 1, 2, SUB, DH), BF),
        pltpu.SemaphoreType.DMA((2, links + 1, 2)), pltpu.SemaphoreType.DMA((2, links + 1, 2)),
        pltpu.SemaphoreType.DMA((2, links + 1, 2)), pltpu.SemaphoreType.DMA((2, links + 1, 2)),
    ]
    return body, scratch


def solution(mesh):
    ctx_n, tp_n = mesh.shape["ctx"], mesh.shape["tp"]
    body, scratch = kernel_body(ctx_n, tp_n)

    def per_device(tokens, feature_weight, window_weight, value_weight, log_decay, out_grad):
        vmem = pl.BlockSpec(memory_space=pltpu.VMEM)
        anywhere = pl.BlockSpec(memory_space=pl.ANY)
        return pl.pallas_call(
            body,
            out_shape=(
                jax.ShapeDtypeStruct((ROWS, DH), BF),
                jax.ShapeDtypeStruct((ROWS, D), BF),
            ),
            in_specs=[anywhere] * 4 + [vmem, vmem],
            out_specs=(vmem, vmem),
            scratch_shapes=scratch,
            compiler_params=pltpu.CompilerParams(
                collective_id=0, has_side_effects=True, vmem_limit_bytes=48 << 20
            ),
            name="layer",
        )(
            tokens, feature_weight, window_weight, value_weight,
            log_decay.reshape(1, ROWS), out_grad,
        )

    in_specs = (
        P("ctx", None), P(None, "tp"), P(None, "tp"), P(None, "tp"),
        P("ctx", "tp"), P("ctx", "tp"),
    )
    return jax.shard_map(
        per_device, mesh=mesh, in_specs=in_specs,
        out_specs=(P("ctx", "tp"), P("ctx", None)), check_vma=False,
    )
```

```python
import jax
import jax.numpy as jnp
from jax import lax
from jax.experimental import pallas as pl
from jax.experimental.pallas import tpu as pltpu
from jax.sharding import PartitionSpec as P

F32 = jnp.float32
BF = jnp.bfloat16
MESH = pl.DeviceIdType.MESH
ROWS = 256
DH = 128
D = 2048
FEATS = 256
HALF = 96
SHARD = 352
SUBS = ((0, 96), (96, 96), (192, 80), (272, 80))
NEG = -1e30


def dot(a, b, ca, cb, precision=None):
    return lax.dot_general(
        a, b, (((ca,), (cb,)), ((), ())), precision=precision, preferred_element_type=F32
    )


def nn(a, b):
    return dot(a, b, 1, 0)


def nt(a, b):
    return dot(a, b, 1, 1)


def tn(a, b):
    return dot(a, b, 0, 0)


def iota(shape, dim):
    return lax.broadcasted_iota(jnp.int32, shape, dim)


def selections(offset):
    row = iota((32, FEATS), 0) - offset
    f = iota((32, FEATS), 1)
    low = f & 15
    pair = f < 136
    linear = (f >= 144) & (f < 160)
    first = (row == low) & (pair | linear)
    second = (row == ((low + (f >> 4)) & 15)) & pair
    return (
        jnp.where(first, 1.0, 0.0).astype(BF),
        jnp.where(second, 1.0, 0.0).astype(BF),
    )


def rate_of(block):
    return block[84:85] + block[85:86]


def with_rate(block, rate):
    row = iota((HALF, DH), 0)
    high = rate.astype(BF).astype(F32)
    return jnp.where(row == 84, high, jnp.where(row == 85, rate - high, block)).astype(BF)


def kernel_body(ctx_n, tp_n):
    ynum, xnum = 8, ctx_n // 16
    links = tp_n // 2
    back = tp_n - 1 - links

    def body(
        tok_h, wf_h, ww_h, wv_h, ld_h, og_h,
        att_ref, res,
        tok, wf, ww, wv, ld_ref, og_ref, insem,
        kv, kvs, kvr,
        msg, pm, hb, yb, rb, xb, pb, po,
        cs, cr, ys, yr, xs, xr,
        dkv0, dkv2, dkv4, dsend, prt, m2, m1, r2, r1, gs, gr,
        part, rsb, rss, rsr, ags, agr,
    ):
        i = lax.axis_index("ctx")
        z = lax.axis_index("tp")
        c = lax.rem(i, 2)
        chip = i // 2
        y = lax.rem(chip, ynum)
        x = chip // ynum
        partner = i + 1 - 2 * c
        after = lax.rem(i + 2, ctx_n)
        before = lax.rem(i + ctx_n - 2, ctx_n)
        up = lax.rem(z + 1, tp_n)
        down = lax.rem(z + tp_n - 1, tp_n)

        def y_peer(k):
            return (x * ynum + lax.rem(y + k + ynum, ynum)) * 2 + c

        def x_peer(k):
            return (lax.rem(x + k + xnum, xnum) * ynum + y) * 2 + c

        loads = [
            pltpu.make_async_copy(a, b, insem.at[n])
            for n, (a, b) in enumerate(
                ((ld_h, ld_ref), (tok_h, tok), (wf_h, wf), (wv_h, wv), (og_h, og_ref), (ww_h, ww))
            )
        ]
        for one in loads:
            one.start()
        barrier = pltpu.get_barrier_semaphore()
        peers = [{"ctx": partner}, {"ctx": after}, {"ctx": before}, {"tp": up}, {"tp": down}]
        peers += [{"ctx": y_peer(k)} for k in range(1, ynum)]
        peers += [{"ctx": x_peer(k)} for k in range(1, xnum)]
        for peer in peers:
            pl.semaphore_signal(barrier, inc=1, device_id=peer, device_id_type=MESH)

        def send(src, dst, ssem, rsem, peer):
            copy = pltpu.make_async_remote_copy(
                src_ref=src, dst_ref=dst, send_sem=ssem, recv_sem=rsem,
                device_id=peer, device_id_type=MESH,
            )
            copy.start()
            return copy

        loads[0].wait()
        ld = jnp.broadcast_to(ld_ref[...], (DH, ROWS))
        tri = jnp.where(iota((ROWS, ROWS), 1) <= iota((ROWS, ROWS), 0), 1.0, 0.0).astype(F32)
        cum = dot(tri, ld, 1, 1, lax.Precision.HIGHEST)
        cum_row = dot(ld[0:8], tri, 1, 1, lax.Precision.HIGHEST)[0:1]
        total = cum[ROWS - 1 : ROWS]
        growth = jnp.exp(cum)
        tail = jnp.exp(total - cum)
        causal = iota((ROWS, ROWS), 1) <= iota((ROWS, ROWS), 0)
        decay = jnp.exp(jnp.where(causal, cum[:, 0:1] - cum_row, NEG))
        tail1 = tail[:, 0:1]
        growth1 = growth[:, 0:1]

        aq, bq = selections(0)
        ak, bk = selections(16)
        lane = iota((1, FEATS), 1)
        a0 = jnp.where(lane == 136, 1.0, 0.0)
        b0 = jnp.where((lane == 136) | ((lane >= 144) & (lane < 160)), 1.0, 0.0)
        wq = jnp.where(lane < 16, 0.5, 1.0)

        for n in range(1, 4):
            loads[n].wait()
        toks = tok[...]
        fs = (nt(toks, wf[...]).astype(BF).astype(F32) * 0.5).astype(BF)
        val = nn(toks, wv[...]).astype(BF)
        ka = nn(fs, ak) + a0
        kb = nn(fs, bk) + b0
        phik = ka * kb * tail1
        phik_b = phik.astype(BF)

        def message(num, den):
            row = iota((16, DH), 0)
            high = total.astype(BF).astype(F32)
            extra = jnp.where(row == 0, den[:, :DH], 0.0)
            extra = jnp.where(row == 1, den[:, DH:], extra)
            extra = jnp.where(row == 4, high, extra)
            extra = jnp.where(row == 5, total - high, extra).astype(BF)
            return jnp.concatenate(
                [num[0:80].astype(BF), extra, num[80:160].astype(BF), extra], axis=0
            )

        def scan_stages(n, cc, yy, xx, sign):
            state = {}

            def start(num, den):
                msg[n] = message(num, den)
                state["a"] = send(msg.at[n], pm.at[n], cs.at[2 * n], cr.at[2 * n], {"ctx": partner})

            def stage_y():
                state["a"].wait()
                own = msg[n, pl.ds(pl.multiple_of(c * HALF, 16), HALF)].astype(F32)
                other = pm[n, pl.ds(pl.multiple_of(c * HALF, 16), HALF)].astype(F32)
                to, tp_ = rate_of(own), rate_of(other)
                first = cc == 0
                both = jnp.where(first, jnp.exp(tp_), 1.0) * own
                both = both + jnp.where(first, 1.0, jnp.exp(to)) * other
                hb[n] = with_rate(both, to + tp_)
                far_first = sorted(range(1, ynum), key=lambda k: -min(k, ynum - k))
                sent = {
                    k: send(hb.at[n], yb.at[n, k], ys.at[n, k], yr.at[n, k], {"ctx": y_peer(sign * k)})
                    for k in far_first
                }
                state["y"] = [sent[k] for k in range(1, ynum)]

            def stage_x():
                prefix = jnp.zeros((HALF, DH), F32)
                suffix = jnp.zeros((HALF, DH), F32)
                d1 = jnp.zeros((1, DH), F32)
                d2 = jnp.zeros((1, DH), F32)
                for k in range(1, ynum):
                    state["y"][k - 1].wait_recv()
                    block = yb[n, k].astype(F32)
                    rate = rate_of(block)
                    early = k <= yy
                    prefix = prefix + jnp.where(early, jnp.exp(d1), 0.0) * block
                    suffix = suffix + jnp.where(early, 0.0, jnp.exp(d2)) * block
                    d1 = d1 + jnp.where(early, rate, 0.0)
                    d2 = d2 + jnp.where(early, 0.0, rate)
                own = hb[n].astype(F32)
                rate = rate_of(own)
                row_sum = jnp.exp(d2) * (jnp.exp(rate) * prefix + own) + suffix
                rb[n] = with_rate(row_sum, d1 + rate + d2)
                state["x"] = [
                    send(rb.at[n], xb.at[n, k], xs.at[n, k], xr.at[n, k], {"ctx": x_peer(sign * k)})
                    for k in range(1, xnum)
                ]
                state["prefix"], state["d1"] = prefix, d1

            def stage_pair():
                rows = jnp.zeros((HALF, DH), F32)
                dx = jnp.zeros((1, DH), F32)
                for k in range(1, xnum):
                    state["x"][k - 1].wait_recv()
                    block = xb[n, k].astype(F32)
                    early = k <= xx
                    rows = rows + jnp.where(early, jnp.exp(dx), 0.0) * block
                    dx = dx + jnp.where(early, rate_of(block), 0.0)
                pb[n] = (state["prefix"] + jnp.exp(state["d1"]) * rows).astype(BF)
                state["b"] = send(
                    pb.at[n], po.at[n], cs.at[2 * n + 1], cr.at[2 * n + 1], {"ctx": partner}
                )

            def finish():
                state["b"].wait()
                for one in state["y"] + state["x"]:
                    one.wait_send()
                mine, theirs = pb[n].astype(F32), po[n].astype(F32)
                low = jnp.where(c == 0, mine, theirs)
                high = jnp.where(c == 0, theirs, mine)
                near = pm[n].astype(F32)
                rate = rate_of(near[0:HALF])
                second = cc == 1
                scale = jnp.where(second, jnp.exp(rate), 1.0)
                take = jnp.where(second, 1.0, 0.0)
                num = jnp.concatenate(
                    [
                        scale * low[0:80] + take * near[0:80],
                        scale * high[0:80] + take * near[96:176],
                        jnp.zeros((FEATS - 160, DH), F32),
                    ],
                    axis=0,
                ).astype(BF)
                dens = scale * low[80:82] + take * near[80:82]
                return num, jnp.concatenate([dens[0:1], dens[1:2]], axis=1)

            return start, stage_y, stage_x, stage_pair, finish

        fwd = scan_stages(0, c, y, x, 1)
        rev = scan_stages(1, 1 - c, ynum - 1 - y, xnum - 1 - x, -1)

        pl.semaphore_wait(barrier, len(peers))
        fwd[0](tn(phik_b, val), jnp.sum(phik, axis=0, keepdims=True))

        loads[4].wait()
        loads[5].wait()
        og = og_ref[...]
        win = nn(toks, ww[...]).astype(BF)
        wquery = win[:, :DH]
        kv[4] = jnp.concatenate([win[:, DH:], val], axis=1)
        fwd[1]()
        hop1 = send(kv.at[4], kv.at[2], kvs.at[0], kvr.at[0], {"ctx": after})

        lane32 = iota((1, 32), 1)
        perm = jnp.where(
            iota((32, 32), 0) == ((iota((32, 32), 1) + 16) & 31), 1.0, 0.0
        ).astype(BF)
        swapped = nn(fs, perm)
        fq = jnp.where(lane32 < 16, fs.astype(F32), 0.0).astype(BF)
        ks = jnp.where(lane32 < 16, swapped, 0.0).astype(BF)
        qs = jnp.where(lane32 < 16, 0.0, swapped).astype(BF)
        prod = nt(fq, ks)
        weights = (1.0 + prod + 0.5 * prod * prod) * decay
        weights_b = weights.astype(BF)
        qa = nn(fs, aq) + a0
        qb = nn(fs, bq) + b0
        phiq = qa * qb * wq
        phiq_b = phiq.astype(BF)

        num_in = nn(weights_b, val)
        den_in = jnp.sum(weights, axis=1, keepdims=True)
        hop1.wait()
        hop2 = send(kv.at[2], kv.at[0], kvs.at[1], kvr.at[1], {"ctx": after})
        pair1 = send(kv.at[4 - 2 * c], kv.at[3], kvs.at[2], kvr.at[2], {"ctx": partner})

        fwd[2]()
        hop2.wait()
        pair2 = send(kv.at[2 - 2 * c], kv.at[1], kvs.at[3], kvr.at[3], {"ctx": partner})
        fwd[3]()
        state_num, state_den = fwd[4]()

        num = num_in + growth * nn(phiq_b, state_num)
        den = den_in + growth1 * jnp.sum(phiq * state_den, axis=1, keepdims=True)
        inv = 1.0 / den
        linear = num * inv
        ogf = og.astype(F32)
        along = jnp.sum(ogf * linear, axis=1, keepdims=True)
        dnum = ogf * inv
        gden = growth1 * (-along * inv)
        gnum = (growth * dnum).astype(BF)
        rev[0](tn(phiq_b, gnum), jnp.sum(phiq * gden, axis=0, keepdims=True))

        pair1.wait()
        pair2.wait()
        scale = DH**-0.5
        scores = []
        for d in range(5):
            s = nt(wquery, kv[4 - d, :, :DH]) * scale
            if d == 0:
                s = jnp.where(causal, s, NEG)
            elif d == 4:
                s = jnp.where(causal | (i < d), NEG, s)
            else:
                s = jnp.where(i < d, NEG, s)
            scores.append(s)
        top = jnp.max(scores[0], axis=1, keepdims=True)
        for s in scores[1:]:
            top = jnp.maximum(top, jnp.max(s, axis=1, keepdims=True))
        probs = [jnp.exp(s - top) for s in scores]
        mass = jnp.sum(probs[0], axis=1, keepdims=True)
        for p in probs[1:]:
            mass = mass + jnp.sum(p, axis=1, keepdims=True)
        imass = 1.0 / mass
        windowed = jnp.zeros((ROWS, DH), F32)
        for d in range(5):
            windowed = windowed + nn(probs[d].astype(BF), kv[4 - d, :, DH:])
        windowed = windowed * imass
        att_ref[...] = (linear + windowed).astype(BF)
        rev[1]()
        delta = jnp.sum(ogf * windowed, axis=1, keepdims=True)
        dquery = jnp.zeros((ROWS, DH), F32)
        local_dv = None
        for d in (1, 3, 4, 2, 0):
            dp = nt(og, kv[4 - d, :, DH:])
            if d == 0:
                local_dv = dp
            p = probs[d] * imass
            ds = (p * (dp - delta) * scale).astype(BF)
            dquery = dquery + nn(ds, kv[4 - d, :, :DH])
            both = jnp.concatenate([tn(ds, wquery), tn(p.astype(BF), og)], axis=1)
            if d == 1:
                dsend[0] = both.astype(BF)
            elif d == 3:
                dsend[1] = both.astype(BF)
                swap = send(dsend, prt, gs.at[0], gr.at[0], {"ctx": partner})
            else:
                {0: dkv0, 2: dkv2, 4: dkv4}[d][...] = both
        rev[2]()

        swap.wait()
        m2[...] = (dkv4[...] + jnp.where(c == 1, prt[1].astype(F32), 0.0)).astype(BF)
        ret2 = send(m2, r2, gs.at[1], gr.at[1], {"ctx": before})

        dw = (local_dv - along) * inv
        dprod = (dw * decay * (1.0 + prod)).astype(BF)
        dphiq = (nt(gnum, state_num) + gden * state_den) * wq
        dfeat = nn(dprod, ks) + tn(dprod, qs)
        dfeat = dfeat + nt((dphiq * qb).astype(BF), aq) + nt((dphiq * qa).astype(BF), bq)
        dval = tn(weights_b, dnum.astype(BF))

        rev[3]()
        ret2.wait()
        near = jnp.where(c == 0, prt[1].astype(F32), prt[0].astype(F32))
        m1[...] = (dkv2[...] + near + r2[...].astype(F32)).astype(BF)
        ret1 = send(m1, r1, gs.at[2], gr.at[2], {"ctx": before})
        back_num, back_den = rev[4]()

        dphik = tail1 * (nt(val, back_num) + back_den)
        dfeat = dfeat + nt((dphik * kb).astype(BF), ak) + nt((dphik * ka).astype(BF), bk)
        dval = dval + nn(phik_b, back_num)
        gfeat = (0.5 * dfeat).astype(BF)
        ret1.wait()
        whole = dkv0[...] + jnp.where(c == 0, prt[0].astype(F32), 0.0) + r1[...].astype(F32)
        gwin = jnp.concatenate([dquery, whole[:, :DH]], axis=1).astype(BF)
        gval = (dval + whole[:, DH:]).astype(BF)

        for j in range(D // DH):
            cut = slice(j * DH, (j + 1) * DH)
            term = nt(gwin, ww[cut]) + nt(gval, wv[cut]) + nn(gfeat, wf[:, cut])
            part[j * ROWS : (j + 1) * ROWS] = term.astype(BF)
        tail_rows = tp_n * SHARD - D // DH * ROWS
        part[D // DH * ROWS :] = jnp.zeros((tail_rows, DH), BF)

        def rows_of(shard, h):
            at = lax.rem(shard + 2 * tp_n, tp_n) * SHARD + SUBS[h][0]
            return pl.ds(pl.multiple_of(at, 16), SUBS[h][1])

        def steps(way, h):
            return links if way == h % 2 else back

        def slot(way, t, h):
            return rsb.at[way, t, h, pl.ds(0, SUBS[h][1])]

        sides = ((0, 1, up), (1, -1, down))
        rs = {}
        ag = {}
        for t in range(1, links + 1):
            for h in range(len(SUBS)):
                for way, sign, peer in sides:
                    last = steps(way, h)
                    if t > last:
                        continue
                    rows = rows_of(z + sign * (last + 1 - t), h)
                    src = part.at[rows]
                    if t > 1:
                        rs[way, t - 1, h].wait_recv()
                        src = slot(way, t - 1, h)
                        src[...] = (src[...].astype(F32) + part[rows].astype(F32)).astype(BF)
                    rs[way, t, h] = send(
                        src, slot(way, t, h), rss.at[way, t, h], rsr.at[way, t, h], {"tp": peer}
                    )
        for t in range(1, links + 1):
            for h in range(len(SUBS)):
                if t == 1:
                    rows = rows_of(z, h)
                    total_in = part[rows].astype(F32)
                    for way, _, _ in sides:
                        rs[way, steps(way, h), h].wait_recv()
                        total_in = total_in + slot(way, steps(way, h), h)[...].astype(F32)
                    res[rows] = total_in.astype(BF)
                for way, sign, peer in sides:
                    if t > steps(way, h):
                        continue
                    if t > 1:
                        ag[way, t - 1, h].wait_recv()
                    rows = rows_of(z - sign * (t - 1), h)
                    ag[way, t, h] = send(
                        res.at[rows], res.at[rows], ags.at[way, t, h], agr.at[way, t, h],
                        {"tp": peer},
                    )
        for h in range(len(SUBS)):
            for way, _, _ in sides:
                ag[way, steps(way, h), h].wait_recv()
        for one in list(rs.values()) + list(ag.values()):
            one.wait_send()

    scratch = [
        pltpu.VMEM((ROWS, D), BF), pltpu.VMEM((32, D), BF),
        pltpu.VMEM((D, 2 * DH), BF), pltpu.VMEM((D, DH), BF),
        pltpu.VMEM((1, ROWS), F32), pltpu.VMEM((ROWS, DH), BF),
        pltpu.SemaphoreType.DMA((6,)),
        pltpu.VMEM((5, ROWS, 2 * DH), BF),
        pltpu.SemaphoreType.DMA((4,)), pltpu.SemaphoreType.DMA((4,)),
        pltpu.VMEM((2, 2 * HALF, DH), BF), pltpu.VMEM((2, 2 * HALF, DH), BF),
        pltpu.VMEM((2, HALF, DH), BF), pltpu.VMEM((2, 8, HALF, DH), BF),
        pltpu.VMEM((2, HALF, DH), BF), pltpu.VMEM((2, 4, HALF, DH), BF),
        pltpu.VMEM((2, HALF, DH), BF), pltpu.VMEM((2, HALF, DH), BF),
        pltpu.SemaphoreType.DMA((4,)), pltpu.SemaphoreType.DMA((4,)),
        pltpu.SemaphoreType.DMA((2, 8)), pltpu.SemaphoreType.DMA((2, 8)),
        pltpu.SemaphoreType.DMA((2, 4)), pltpu.SemaphoreType.DMA((2, 4)),
        pltpu.VMEM((ROWS, 2 * DH), F32), pltpu.VMEM((ROWS, 2 * DH), F32),
        pltpu.VMEM((ROWS, 2 * DH), F32),
        pltpu.VMEM((2, ROWS, 2 * DH), BF), pltpu.VMEM((2, ROWS, 2 * DH), BF),
        pltpu.VMEM((ROWS, 2 * DH), BF), pltpu.VMEM((ROWS, 2 * DH), BF),
        pltpu.VMEM((ROWS, 2 * DH), BF), pltpu.VMEM((ROWS, 2 * DH), BF),
        pltpu.SemaphoreType.DMA((3,)), pltpu.SemaphoreType.DMA((3,)),
        pltpu.VMEM((tp_n * SHARD, DH), BF),
        pltpu.VMEM((2, links + 1, len(SUBS), SUBS[0][1], DH), BF),
        pltpu.SemaphoreType.DMA((2, links + 1, len(SUBS))), pltpu.SemaphoreType.DMA((2, links + 1, len(SUBS))),
        pltpu.SemaphoreType.DMA((2, links + 1, len(SUBS))), pltpu.SemaphoreType.DMA((2, links + 1, len(SUBS))),
    ]
    return body, scratch


def write_out(att_ref, res_ref, att_h, ig_h, sem):
    copies = [
        pltpu.make_async_copy(
            res_ref.at[pl.ds(j * ROWS, ROWS)], ig_h.at[:, pl.ds(j * DH, DH)], sem.at[j]
        )
        for j in range(D // DH)
    ]
    copies.append(pltpu.make_async_copy(att_ref, att_h, sem.at[D // DH]))
    for one in copies:
        one.start()
    for one in copies:
        one.wait()


def solution(mesh):
    ctx_n, tp_n = mesh.shape["ctx"], mesh.shape["tp"]
    body, scratch = kernel_body(ctx_n, tp_n)
    vmem = pl.BlockSpec(memory_space=pltpu.VMEM)
    hbm = pl.BlockSpec(memory_space=pltpu.HBM)

    def per_device(tokens, feature_weight, window_weight, value_weight, log_decay, out_grad):
        attended, packed = pl.pallas_call(
            body,
            out_shape=(
                jax.ShapeDtypeStruct((ROWS, DH), BF),
                jax.ShapeDtypeStruct((tp_n * SHARD, DH), BF),
            ),
            in_specs=[hbm] * 6,
            out_specs=(vmem, vmem),
            scratch_shapes=scratch,
            compiler_params=pltpu.CompilerParams(
                collective_id=0, has_side_effects=True, vmem_limit_bytes=48 << 20
            ),
            name="layer",
        )(*(
            pltpu.with_memory_space_constraint(a, pltpu.HBM)
            for a in (
                tokens, feature_weight.T, window_weight, value_weight,
                log_decay.reshape(1, ROWS), out_grad,
            )
        ))
        return pl.pallas_call(
            write_out,
            out_shape=(
                jax.ShapeDtypeStruct((ROWS, DH), BF),
                jax.ShapeDtypeStruct((ROWS, D), BF),
            ),
            in_specs=[vmem, vmem],
            out_specs=(hbm, hbm),
            scratch_shapes=[pltpu.SemaphoreType.DMA((D // DH + 1,))],
            compiler_params=pltpu.CompilerParams(vmem_limit_bytes=8 << 20),
            name="write_out",
        )(attended, packed)

    in_specs = (
        P("ctx", None), P(None, "tp"), P(None, "tp"), P(None, "tp"),
        P("ctx", "tp"), P("ctx", "tp"),
    )
    return jax.shard_map(
        per_device, mesh=mesh, in_specs=in_specs,
        out_specs=(P("ctx", "tp"), P("ctx", None)), check_vma=False,
    )
```

```python
import jax
import jax.numpy as jnp
from jax import lax
from jax.experimental import pallas as pl
from jax.experimental.pallas import tpu as pltpu
from jax.sharding import PartitionSpec as P

F32 = jnp.float32
BF = jnp.bfloat16
MESH = pl.DeviceIdType.MESH
ROWS = 256
DH = 128
D = 2048
FEATS = 256
HALF = 96
SHARD = 352
SUBS = ((0, 96), (96, 96), (192, 80), (272, 80))
NEG = -1e30


def dot(a, b, ca, cb, precision=None):
    return lax.dot_general(
        a, b, (((ca,), (cb,)), ((), ())), precision=precision, preferred_element_type=F32
    )


def nn(a, b):
    return dot(a, b, 1, 0)


def nt(a, b):
    return dot(a, b, 1, 1)


def tn(a, b):
    return dot(a, b, 0, 0)


def iota(shape, dim):
    return lax.broadcasted_iota(jnp.int32, shape, dim)


def selections(offset):
    row = iota((32, FEATS), 0) - offset
    f = iota((32, FEATS), 1)
    low = f & 15
    pair = f < 136
    linear = (f >= 144) & (f < 160)
    first = (row == low) & (pair | linear)
    second = (row == ((low + (f >> 4)) & 15)) & pair
    return (
        jnp.where(first, 1.0, 0.0).astype(BF),
        jnp.where(second, 1.0, 0.0).astype(BF),
    )


def rate_of(block):
    return block[84:85] + block[85:86]


def with_rate(block, rate):
    row = iota((HALF, DH), 0)
    high = rate.astype(BF).astype(F32)
    return jnp.where(row == 84, high, jnp.where(row == 85, rate - high, block)).astype(BF)


def kernel_body(ctx_n, tp_n):
    ynum, xnum = 8, ctx_n // 16
    links = tp_n // 2
    back = tp_n - 1 - links

    def body(
        tok_h, wf_h, ww_h, wv_h, ld_h, og_h,
        att_ref, res,
        tok, wf, ww, wv, ld_ref, og_ref, insem,
        kv, kvs, kvr,
        msg, pm, hb, yb, rb, xb, pb, po,
        cs, cr, ys, yr, xs, xr,
        dkv0, dkv2, dkv4, dsend, prt, m2, m1, r2, r1, gs, gr,
        part, rsb, rss, rsr, ags, agr,
    ):
        i = lax.axis_index("ctx")
        z = lax.axis_index("tp")
        c = lax.rem(i, 2)
        chip = i // 2
        y = lax.rem(chip, ynum)
        x = chip // ynum
        partner = i + 1 - 2 * c
        after = lax.rem(i + 2, ctx_n)
        before = lax.rem(i + ctx_n - 2, ctx_n)
        up = lax.rem(z + 1, tp_n)
        down = lax.rem(z + tp_n - 1, tp_n)

        def y_peer(k):
            return (x * ynum + lax.rem(y + k + ynum, ynum)) * 2 + c

        def x_peer(k):
            return (lax.rem(x + k + xnum, xnum) * ynum + y) * 2 + c

        loads = [
            pltpu.make_async_copy(a, b, insem.at[n])
            for n, (a, b) in enumerate(
                ((ld_h, ld_ref), (tok_h, tok), (wf_h, wf), (wv_h, wv), (og_h, og_ref), (ww_h, ww))
            )
        ]
        for one in loads:
            one.start()
        barrier = pltpu.get_barrier_semaphore()
        peers = [{"ctx": partner}, {"ctx": after}, {"ctx": before}, {"tp": up}, {"tp": down}]
        peers += [{"ctx": y_peer(k)} for k in range(1, ynum)]
        peers += [{"ctx": x_peer(k)} for k in range(1, xnum)]
        for peer in peers:
            pl.semaphore_signal(barrier, inc=1, device_id=peer, device_id_type=MESH)

        def send(src, dst, ssem, rsem, peer):
            copy = pltpu.make_async_remote_copy(
                src_ref=src, dst_ref=dst, send_sem=ssem, recv_sem=rsem,
                device_id=peer, device_id_type=MESH,
            )
            copy.start()
            return copy

        loads[0].wait()
        ld = jnp.broadcast_to(ld_ref[...], (DH, ROWS))
        tri = jnp.where(iota((ROWS, ROWS), 1) <= iota((ROWS, ROWS), 0), 1.0, 0.0).astype(F32)
        cum = dot(tri, ld, 1, 1, lax.Precision.HIGHEST)
        cum_row = dot(ld[0:8], tri, 1, 1, lax.Precision.HIGHEST)[0:1]
        total = cum[ROWS - 1 : ROWS]
        growth = jnp.exp(cum)
        tail = jnp.exp(total - cum)
        causal = iota((ROWS, ROWS), 1) <= iota((ROWS, ROWS), 0)
        decay = jnp.exp(jnp.where(causal, cum[:, 0:1] - cum_row, NEG))
        tail1 = tail[:, 0:1]
        growth1 = growth[:, 0:1]

        aq, bq = selections(0)
        ak, bk = selections(16)
        lane = iota((1, FEATS), 1)
        a0 = jnp.where(lane == 136, 1.0, 0.0)
        b0 = jnp.where((lane == 136) | ((lane >= 144) & (lane < 160)), 1.0, 0.0)
        wq = jnp.where(lane < 16, 0.5, 1.0)

        for n in range(1, 4):
            loads[n].wait()
        toks = tok[...]
        fs = (nt(toks, wf[...]).astype(BF).astype(F32) * 0.5).astype(BF)
        val = nn(toks, wv[...]).astype(BF)
        ka = nn(fs, ak) + a0
        kb = nn(fs, bk) + b0
        phik = ka * kb * tail1
        phik_b = phik.astype(BF)

        def message(num, den):
            row = iota((16, DH), 0)
            high = total.astype(BF).astype(F32)
            extra = jnp.where(row == 0, den[:, :DH], 0.0)
            extra = jnp.where(row == 1, den[:, DH:], extra)
            extra = jnp.where(row == 4, high, extra)
            extra = jnp.where(row == 5, total - high, extra).astype(BF)
            return jnp.concatenate(
                [num[0:80].astype(BF), extra, num[80:160].astype(BF), extra], axis=0
            )

        def scan_stages(n, cc, yy, xx, sign):
            state = {}

            def start(num, den):
                msg[n] = message(num, den)
                state["a"] = send(msg.at[n], pm.at[n], cs.at[2 * n], cr.at[2 * n], {"ctx": partner})

            def stage_y():
                state["a"].wait()
                own = msg[n, pl.ds(pl.multiple_of(c * HALF, 16), HALF)].astype(F32)
                other = pm[n, pl.ds(pl.multiple_of(c * HALF, 16), HALF)].astype(F32)
                to, tp_ = rate_of(own), rate_of(other)
                first = cc == 0
                both = jnp.where(first, jnp.exp(tp_), 1.0) * own
                both = both + jnp.where(first, 1.0, jnp.exp(to)) * other
                hb[n] = with_rate(both, to + tp_)
                far_first = sorted(range(1, ynum), key=lambda k: -min(k, ynum - k))
                sent = {
                    k: send(hb.at[n], yb.at[n, k], ys.at[n, k], yr.at[n, k], {"ctx": y_peer(sign * k)})
                    for k in far_first
                }
                state["y"] = [sent[k] for k in range(1, ynum)]

            def stage_x():
                prefix = jnp.zeros((HALF, DH), F32)
                suffix = jnp.zeros((HALF, DH), F32)
                d1 = jnp.zeros((1, DH), F32)
                d2 = jnp.zeros((1, DH), F32)
                for k in range(1, ynum):
                    state["y"][k - 1].wait_recv()
                    block = yb[n, k].astype(F32)
                    rate = rate_of(block)
                    early = k <= yy
                    prefix = prefix + jnp.where(early, jnp.exp(d1), 0.0) * block
                    suffix = suffix + jnp.where(early, 0.0, jnp.exp(d2)) * block
                    d1 = d1 + jnp.where(early, rate, 0.0)
                    d2 = d2 + jnp.where(early, 0.0, rate)
                own = hb[n].astype(F32)
                rate = rate_of(own)
                row_sum = jnp.exp(d2) * (jnp.exp(rate) * prefix + own) + suffix
                rb[n] = with_rate(row_sum, d1 + rate + d2)
                state["x"] = [
                    send(rb.at[n], xb.at[n, k], xs.at[n, k], xr.at[n, k], {"ctx": x_peer(sign * k)})
                    for k in range(1, xnum)
                ]
                state["prefix"], state["d1"] = prefix, d1

            def stage_pair():
                rows = jnp.zeros((HALF, DH), F32)
                dx = jnp.zeros((1, DH), F32)
                for k in range(1, xnum):
                    state["x"][k - 1].wait_recv()
                    block = xb[n, k].astype(F32)
                    early = k <= xx
                    rows = rows + jnp.where(early, jnp.exp(dx), 0.0) * block
                    dx = dx + jnp.where(early, rate_of(block), 0.0)
                pb[n] = (state["prefix"] + jnp.exp(state["d1"]) * rows).astype(BF)
                state["b"] = send(
                    pb.at[n], po.at[n], cs.at[2 * n + 1], cr.at[2 * n + 1], {"ctx": partner}
                )

            def finish():
                state["b"].wait()
                for one in state["y"] + state["x"]:
                    one.wait_send()
                mine, theirs = pb[n].astype(F32), po[n].astype(F32)
                low = jnp.where(c == 0, mine, theirs)
                high = jnp.where(c == 0, theirs, mine)
                near = pm[n].astype(F32)
                rate = rate_of(near[0:HALF])
                second = cc == 1
                scale = jnp.where(second, jnp.exp(rate), 1.0)
                take = jnp.where(second, 1.0, 0.0)
                num = jnp.concatenate(
                    [
                        scale * low[0:80] + take * near[0:80],
                        scale * high[0:80] + take * near[96:176],
                        jnp.zeros((FEATS - 160, DH), F32),
                    ],
                    axis=0,
                ).astype(BF)
                dens = scale * low[80:82] + take * near[80:82]
                return num, jnp.concatenate([dens[0:1], dens[1:2]], axis=1)

            return start, stage_y, stage_x, stage_pair, finish

        fwd = scan_stages(0, c, y, x, 1)
        rev = scan_stages(1, 1 - c, ynum - 1 - y, xnum - 1 - x, -1)

        pl.semaphore_wait(barrier, len(peers))
        fwd[0](tn(phik_b, val), jnp.sum(phik, axis=0, keepdims=True))

        loads[4].wait()
        loads[5].wait()
        og = og_ref[...]
        win = nn(toks, ww[...]).astype(BF)
        wquery = win[:, :DH]
        kv[4] = jnp.concatenate([win[:, DH:], val], axis=1)
        fwd[1]()
        hop1 = send(kv.at[4], kv.at[2], kvs.at[0], kvr.at[0], {"ctx": after})

        lane32 = iota((1, 32), 1)
        perm = jnp.where(
            iota((32, 32), 0) == ((iota((32, 32), 1) + 16) & 31), 1.0, 0.0
        ).astype(BF)
        swapped = nn(fs, perm)
        fq = jnp.where(lane32 < 16, fs.astype(F32), 0.0).astype(BF)
        ks = jnp.where(lane32 < 16, swapped, 0.0).astype(BF)
        qs = jnp.where(lane32 < 16, 0.0, swapped).astype(BF)
        prod = nt(fq, ks)
        weights = (1.0 + prod + 0.5 * prod * prod) * decay
        weights_b = weights.astype(BF)
        qa = nn(fs, aq) + a0
        qb = nn(fs, bq) + b0
        phiq = qa * qb * wq
        phiq_b = phiq.astype(BF)

        num_in = nn(weights_b, val)
        den_in = jnp.sum(weights, axis=1, keepdims=True)
        hop1.wait()
        hop2 = send(kv.at[2], kv.at[0], kvs.at[1], kvr.at[1], {"ctx": after})
        pair1 = send(kv.at[4 - 2 * c], kv.at[3], kvs.at[2], kvr.at[2], {"ctx": partner})

        fwd[2]()
        hop2.wait()
        pair2 = send(kv.at[2 - 2 * c], kv.at[1], kvs.at[3], kvr.at[3], {"ctx": partner})
        fwd[3]()
        state_num, state_den = fwd[4]()

        num = num_in + growth * nn(phiq_b, state_num)
        den = den_in + growth1 * jnp.sum(phiq * state_den, axis=1, keepdims=True)
        inv = 1.0 / den
        linear = num * inv
        ogf = og.astype(F32)
        along = jnp.sum(ogf * linear, axis=1, keepdims=True)
        dnum = ogf * inv
        gden = growth1 * (-along * inv)
        gnum = (growth * dnum).astype(BF)
        rev[0](tn(phiq_b, gnum), jnp.sum(phiq * gden, axis=0, keepdims=True))

        pair1.wait()
        pair2.wait()
        scale = DH**-0.5
        scores = []
        for d in range(5):
            s = nt(wquery, kv[4 - d, :, :DH]) * scale
            if d == 0:
                s = jnp.where(causal, s, NEG)
            elif d == 4:
                s = jnp.where(causal | (i < d), NEG, s)
            else:
                s = jnp.where(i < d, NEG, s)
            scores.append(s)
        top = jnp.max(scores[0], axis=1, keepdims=True)
        for s in scores[1:]:
            top = jnp.maximum(top, jnp.max(s, axis=1, keepdims=True))
        probs = [jnp.exp(s - top) for s in scores]
        mass = jnp.sum(probs[0], axis=1, keepdims=True)
        for p in probs[1:]:
            mass = mass + jnp.sum(p, axis=1, keepdims=True)
        imass = 1.0 / mass
        windowed = jnp.zeros((ROWS, DH), F32)
        for d in range(5):
            windowed = windowed + nn(probs[d].astype(BF), kv[4 - d, :, DH:])
        windowed = windowed * imass
        att_ref[...] = (linear + windowed).astype(BF)
        rev[1]()
        delta = jnp.sum(ogf * windowed, axis=1, keepdims=True)
        dquery = jnp.zeros((ROWS, DH), F32)
        local_dv = None
        for d in (1, 3, 4, 2, 0):
            dp = nt(og, kv[4 - d, :, DH:])
            if d == 0:
                local_dv = dp
            p = probs[d] * imass
            ds = (p * (dp - delta) * scale).astype(BF)
            dquery = dquery + nn(ds, kv[4 - d, :, :DH])
            both = jnp.concatenate([tn(ds, wquery), tn(p.astype(BF), og)], axis=1)
            if d == 1:
                dsend[0] = both.astype(BF)
            elif d == 3:
                dsend[1] = both.astype(BF)
                swap = send(dsend, prt, gs.at[0], gr.at[0], {"ctx": partner})
            else:
                {0: dkv0, 2: dkv2, 4: dkv4}[d][...] = both
        rev[2]()

        swap.wait()
        m2[...] = (dkv4[...] + jnp.where(c == 1, prt[1].astype(F32), 0.0)).astype(BF)
        ret2 = send(m2, r2, gs.at[1], gr.at[1], {"ctx": before})

        dw = (local_dv - along) * inv
        dprod = (dw * decay * (1.0 + prod)).astype(BF)
        dphiq = (nt(gnum, state_num) + gden * state_den) * wq
        dfeat = nn(dprod, ks) + tn(dprod, qs)
        dfeat = dfeat + nt((dphiq * qb).astype(BF), aq) + nt((dphiq * qa).astype(BF), bq)
        dval = tn(weights_b, dnum.astype(BF))

        rev[3]()
        ret2.wait()
        near = jnp.where(c == 0, prt[1].astype(F32), prt[0].astype(F32))
        m1[...] = (dkv2[...] + near + r2[...].astype(F32)).astype(BF)
        ret1 = send(m1, r1, gs.at[2], gr.at[2], {"ctx": before})
        back_num, back_den = rev[4]()

        dphik = tail1 * (nt(val, back_num) + back_den)
        dfeat = dfeat + nt((dphik * kb).astype(BF), ak) + nt((dphik * ka).astype(BF), bk)
        dval = dval + nn(phik_b, back_num)
        gfeat = (0.5 * dfeat).astype(BF)
        ret1.wait()
        whole = dkv0[...] + jnp.where(c == 0, prt[0].astype(F32), 0.0) + r1[...].astype(F32)
        gwin = jnp.concatenate([dquery, whole[:, :DH]], axis=1).astype(BF)
        gval = (dval + whole[:, DH:]).astype(BF)

        for j in range(D // DH):
            cut = slice(j * DH, (j + 1) * DH)
            term = nt(gwin, ww[cut]) + nt(gval, wv[cut]) + nn(gfeat, wf[:, cut])
            part[j * ROWS : (j + 1) * ROWS] = term.astype(BF)
        tail_rows = tp_n * SHARD - D // DH * ROWS
        part[D // DH * ROWS :] = jnp.zeros((tail_rows, DH), BF)

        def rows_of(shard, h):
            at = lax.rem(shard + 2 * tp_n, tp_n) * SHARD + SUBS[h][0]
            return pl.ds(pl.multiple_of(at, 16), SUBS[h][1])

        def steps(way, h):
            return links if way == h % 2 else back

        def slot(way, t, h):
            return rsb.at[way, t, h, pl.ds(0, SUBS[h][1])]

        sides = ((0, 1, up), (1, -1, down))
        rs = {}
        ag = {}
        sent_early = set()
        for t in range(1, links + 1):
            for h in range(len(SUBS)):
                for way, sign, peer in sides:
                    last = steps(way, h)
                    if t > last:
                        continue
                    rows = rows_of(z + sign * (last + 1 - t), h)
                    src = part.at[rows]
                    if t > 1:
                        rs[way, t - 1, h].wait_recv()
                        src = slot(way, t - 1, h)
                        src[...] = (src[...].astype(F32) + part[rows].astype(F32)).astype(BF)
                    rs[way, t, h] = send(
                        src, slot(way, t, h), rss.at[way, t, h], rsr.at[way, t, h], {"tp": peer}
                    )
        finals = {(way, h): rs[way, steps(way, h), h] for way in range(2) for h in range(len(SUBS))}
        for t in range(1, links + 1):
            for h in range(len(SUBS)):
                if t == 1:
                    rows = rows_of(z, h)
                    total_in = part[rows].astype(F32)
                    for way, _, _ in sides:
                        finals[way, h].wait_recv()
                        total_in = total_in + slot(way, steps(way, h), h)[...].astype(F32)
                    res[rows] = total_in.astype(BF)
                for way, sign, peer in sides:
                    if t > steps(way, h):
                        continue
                    if t > 1:
                        ag[way, t - 1, h].wait_recv()
                    rows = rows_of(z - sign * (t - 1), h)
                    ag[way, t, h] = send(
                        res.at[rows], res.at[rows], ags.at[way, t, h], agr.at[way, t, h],
                        {"tp": peer},
                    )
                for way in range(2):
                    done = [rs.pop((way, t, h), None)]
                    if t > 1:
                        done.append(ag.get((way, t - 1, h)))
                        sent_early.add((way, t - 1, h))
                    for one in done:
                        if one is not None:
                            one.wait_send()
        for h in range(len(SUBS)):
            for way, _, _ in sides:
                ag[way, steps(way, h), h].wait_recv()
        for key in ag:
            if key not in sent_early:
                ag[key].wait_send()

    scratch = [
        pltpu.VMEM((ROWS, D), BF), pltpu.VMEM((32, D), BF),
        pltpu.VMEM((D, 2 * DH), BF), pltpu.VMEM((D, DH), BF),
        pltpu.VMEM((1, ROWS), F32), pltpu.VMEM((ROWS, DH), BF),
        pltpu.SemaphoreType.DMA((6,)),
        pltpu.VMEM((5, ROWS, 2 * DH), BF),
        pltpu.SemaphoreType.DMA((4,)), pltpu.SemaphoreType.DMA((4,)),
        pltpu.VMEM((2, 2 * HALF, DH), BF), pltpu.VMEM((2, 2 * HALF, DH), BF),
        pltpu.VMEM((2, HALF, DH), BF), pltpu.VMEM((2, 8, HALF, DH), BF),
        pltpu.VMEM((2, HALF, DH), BF), pltpu.VMEM((2, 4, HALF, DH), BF),
        pltpu.VMEM((2, HALF, DH), BF), pltpu.VMEM((2, HALF, DH), BF),
        pltpu.SemaphoreType.DMA((4,)), pltpu.SemaphoreType.DMA((4,)),
        pltpu.SemaphoreType.DMA((2, 8)), pltpu.SemaphoreType.DMA((2, 8)),
        pltpu.SemaphoreType.DMA((2, 4)), pltpu.SemaphoreType.DMA((2, 4)),
        pltpu.VMEM((ROWS, 2 * DH), F32), pltpu.VMEM((ROWS, 2 * DH), F32),
        pltpu.VMEM((ROWS, 2 * DH), F32),
        pltpu.VMEM((2, ROWS, 2 * DH), BF), pltpu.VMEM((2, ROWS, 2 * DH), BF),
        pltpu.VMEM((ROWS, 2 * DH), BF), pltpu.VMEM((ROWS, 2 * DH), BF),
        pltpu.VMEM((ROWS, 2 * DH), BF), pltpu.VMEM((ROWS, 2 * DH), BF),
        pltpu.SemaphoreType.DMA((3,)), pltpu.SemaphoreType.DMA((3,)),
        pltpu.VMEM((tp_n * SHARD, DH), BF),
        pltpu.VMEM((2, links + 1, len(SUBS), SUBS[0][1], DH), BF),
        pltpu.SemaphoreType.DMA((2, links + 1, len(SUBS))), pltpu.SemaphoreType.DMA((2, links + 1, len(SUBS))),
        pltpu.SemaphoreType.DMA((2, links + 1, len(SUBS))), pltpu.SemaphoreType.DMA((2, links + 1, len(SUBS))),
    ]
    return body, scratch


def write_out(att_ref, res_ref, att_h, ig_h, sem):
    copies = [
        pltpu.make_async_copy(
            res_ref.at[pl.ds(j * ROWS, ROWS)], ig_h.at[:, pl.ds(j * DH, DH)], sem.at[j]
        )
        for j in range(D // DH)
    ]
    copies.append(pltpu.make_async_copy(att_ref, att_h, sem.at[D // DH]))
    for one in copies:
        one.start()
    for one in copies:
        one.wait()


def solution(mesh):
    ctx_n, tp_n = mesh.shape["ctx"], mesh.shape["tp"]
    body, scratch = kernel_body(ctx_n, tp_n)
    vmem = pl.BlockSpec(memory_space=pltpu.VMEM)
    hbm = pl.BlockSpec(memory_space=pltpu.HBM)

    def per_device(tokens, feature_weight, window_weight, value_weight, log_decay, out_grad):
        attended, packed = pl.pallas_call(
            body,
            out_shape=(
                jax.ShapeDtypeStruct((ROWS, DH), BF),
                jax.ShapeDtypeStruct((tp_n * SHARD, DH), BF),
            ),
            in_specs=[hbm] * 6,
            out_specs=(vmem, vmem),
            scratch_shapes=scratch,
            compiler_params=pltpu.CompilerParams(
                collective_id=0, has_side_effects=True, vmem_limit_bytes=48 << 20
            ),
            name="layer",
        )(*(
            pltpu.with_memory_space_constraint(a, pltpu.HBM)
            for a in (
                tokens, feature_weight.T, window_weight, value_weight,
                log_decay.reshape(1, ROWS), out_grad,
            )
        ))
        return pl.pallas_call(
            write_out,
            out_shape=(
                jax.ShapeDtypeStruct((ROWS, DH), BF),
                jax.ShapeDtypeStruct((ROWS, D), BF),
            ),
            in_specs=[vmem, vmem],
            out_specs=(hbm, hbm),
            scratch_shapes=[pltpu.SemaphoreType.DMA((D // DH + 1,))],
            compiler_params=pltpu.CompilerParams(vmem_limit_bytes=8 << 20),
            name="write_out",
        )(attended, packed)

    in_specs = (
        P("ctx", None), P(None, "tp"), P(None, "tp"), P(None, "tp"),
        P("ctx", "tp"), P("ctx", "tp"),
    )
    return jax.shard_map(
        per_device, mesh=mesh, in_specs=in_specs,
        out_specs=(P("ctx", "tp"), P("ctx", None)), check_vma=False,
    )
```
